32 devices in a mesh: row: 4 (over y, x), col: 4 (over z), dp: 2 (over core).
Axes of the slice: x: 2, y: 2, z: 4, core: 2. Of those that a mesh axis runs over, the one named last changes fastest.
Arguments:
- tokens: bfloat16 [512, 8192], P(('row', 'dp'), 'col'), may hold values from -6 to 6
- upstream: bfloat16 [512, 8192], P(('row', 'dp'), 'col'), may hold values from -1.5 to 1.5
- w_gate: bfloat16 [8192, 14336], P('col', 'row'), may hold values from -0.0625 to 0.0625
- w_up: bfloat16 [8192, 14336], P('col', 'row'), may hold values from -0.0625 to 0.0625
- w_down: bfloat16 [14336, 8192], P('row', 'col'), may hold values from -0.046875 to 0.046875
- delta_gate: bfloat16 [4, 4, 192, 128, 128], P('col', 'row'), may hold values from -0.03125 to 0.03125
- delta_up: bfloat16 [4, 4, 192, 128, 128], P('col', 'row'), may hold values from -0.03125 to 0.03125
- delta_down: bfloat16 [4, 4, 192, 128, 128], P('row', 'col'), may hold values from -0.0234375 to 0.0234375
- pattern_gate: int32 [4, 4, 192], P('col', 'row'), may hold values from 0 to 448, as said below
- pattern_up: int32 [4, 4, 192], P('col', 'row'), may hold values from 0 to 448, as said below
- pattern_down: int32 [4, 4, 192], P('row', 'col'), may hold values from 0 to 448, as said below
Outputs:
- output: bfloat16 [512, 8192], P(('row', 'dp'), 'col')
- input_grad: bfloat16 [512, 8192], P(('row', 'dp'), 'col')
- delta_grad_gate: float32 [4, 4, 192, 128, 128], P('col', 'row', 'dp')
- delta_grad_up: float32 [4, 4, 192, 128, 128], P('col', 'row', 'dp')
- delta_grad_down: float32 [4, 4, 192, 128, 128], P('row', 'col', 'dp')
The draws below stay inside these ranges and needn't reach their ends.
Inputs may be any that keep to these rules, and one draw needn't show every extreme that they name: `pattern_gate`: in each tile the 192 slots name distinct blocks of that tile; the value 448 marks an empty slot; live slots come first, a tile holds 48 to 192 of them, and some tile holds 192. `pattern_up`: as for pattern_gate. `pattern_down`: as for pattern_gate.
All inputs are finite; a program needn't handle non-finite values.
Results may differ from the reference program's by a relative error of at most 0.0058.
Values may be sent and summed in bfloat16 or wider, within the bound.
A program may use at most 320 MiB of HBM per device.

```python
import jax
import jax.numpy as jnp
from jax import lax

D = 8192
FF = 14336
BLK = 128
TOKENS = 512
TILE_BLOCKS = 448
CAP = 192
N_ROW = 4
N_COL = 4


def make_pattern(base_key, tiles_first, tiles_second):
    count_key, full_key, score_key = jax.random.split(base_key, 3)
    tile_total = tiles_first * tiles_second
    counts = jax.random.randint(count_key, (tile_total,), CAP // 4, CAP + 1, dtype=jnp.int32)
    filled = jax.random.randint(full_key, (), 0, tile_total, dtype=jnp.int32)
    counts = jnp.where(jnp.arange(tile_total, dtype=jnp.int32) == filled, CAP, counts)
    scores = jax.random.randint(score_key, (tile_total, TILE_BLOCKS), 0, 1 << 20, dtype=jnp.int32) * TILE_BLOCKS
    scores = scores + jnp.arange(TILE_BLOCKS, dtype=jnp.int32)[None, :]
    ranking = jnp.argsort(scores, axis=1, stable=True).astype(jnp.int32)
    chosen = ranking[:, :CAP]
    live = jnp.arange(CAP, dtype=jnp.int32)[None, :] < counts[:, None]
    pattern = jnp.where(live, chosen, TILE_BLOCKS)
    return pattern.reshape(tiles_first, tiles_second, CAP).astype(jnp.int32)


def draw_pattern_gate(key, part):
    return make_pattern(jax.random.fold_in(key, 11), N_COL, N_ROW)


def draw_pattern_up(key, part):
    return make_pattern(jax.random.fold_in(key, 12), N_COL, N_ROW)


def draw_pattern_down(key, part):
    return make_pattern(jax.random.fold_in(key, 13), N_ROW, N_COL)


def block_scale(rng, dims, cuts, smallest, largest):
    gain, own = 1.0, jax.random.fold_in(rng, 6)
    for dim, blocks in cuts:
        heights = jnp.exp(jax.random.uniform(jax.random.fold_in(own, dim), (blocks,), jnp.float32, smallest / len(cuts), largest / len(cuts)))
        gain = gain * jnp.repeat(heights, dims[dim] // blocks).reshape([-1 if axis == dim else 1 for axis in range(len(dims))])
    return gain


def gaussian(key, shape, scale, reach, shards=(), held_as=jnp.bfloat16):
    entries = scale * jax.random.normal(key, shape, jnp.float32)
    if shards:
        entries = entries * block_scale(key, shape, shards, -0.22, 0.18)
    return jnp.clip(entries, -reach, reach).astype(held_as)


def setup_inputs(seed: int = 0) -> dict:
    arg_keys = jax.random.split(jax.random.key(seed), 12)
    tokens = gaussian(arg_keys[0], (TOKENS, D), 1.0, 6.0, ((0, 8), (1, 4)))
    upstream = gaussian(arg_keys[1], (TOKENS, D), 0.25, 1.5, ((0, 8), (1, 4)))
    w_gate = gaussian(arg_keys[2], (D, FF), D ** -0.5, 0.0625, ((0, 4), (1, 4)))
    w_up = gaussian(arg_keys[3], (D, FF), D ** -0.5, 0.0625, ((0, 4), (1, 4)))
    w_down = gaussian(arg_keys[4], (FF, D), FF ** -0.5, 0.046875, ((0, 4), (1, 4)))
    delta_gate = gaussian(arg_keys[5], (N_COL, N_ROW, CAP, BLK, BLK), (4 * D) ** -0.5, 0.03125, ((0, 4), (1, 4)))
    delta_up = gaussian(arg_keys[6], (N_COL, N_ROW, CAP, BLK, BLK), (4 * D) ** -0.5, 0.03125, ((0, 4), (1, 4)))
    delta_down = gaussian(arg_keys[7], (N_ROW, N_COL, CAP, BLK, BLK), (4 * FF) ** -0.5, 0.0234375, ((0, 4), (1, 4)))
    pattern_gate = draw_pattern_gate(jax.random.fold_in(arg_keys[11], 71), 0)
    pattern_up = draw_pattern_up(jax.random.fold_in(arg_keys[11], 71), 0)
    pattern_down = draw_pattern_down(jax.random.fold_in(arg_keys[11], 71), 0)
    return {"tokens": tokens, "upstream": upstream, "w_gate": w_gate, "w_up": w_up, "w_down": w_down, "delta_gate": delta_gate, "delta_up": delta_up, "delta_down": delta_down, "pattern_gate": pattern_gate, "pattern_up": pattern_up, "pattern_down": pattern_down}


def fold_whole(weight, blocks, pattern):
    tiles_first = blocks.shape[0]
    tiles_second = blocks.shape[1]
    block_size = blocks.shape[3]
    per_first = weight.shape[0] // (tiles_first * block_size)
    per_second = weight.shape[1] // (tiles_second * block_size)
    numbers = jnp.arange(per_first * per_second, dtype=jnp.int32)
    one_hot = (pattern[..., None] == numbers).astype(jnp.float32)
    placed = jnp.einsum("absk,absij->abkij", one_hot, blocks.astype(jnp.float32))
    placed = placed.reshape(tiles_first, tiles_second, per_first, per_second, block_size, block_size)
    placed = placed.transpose(0, 2, 4, 1, 3, 5).reshape(weight.shape)
    return (weight.astype(jnp.float32) + placed).astype(jnp.bfloat16)


def block_grads(left_rows, right_rows, pattern):
    tiles_first = pattern.shape[0]
    tiles_second = pattern.shape[1]
    block_size = BLK
    per_first = left_rows.shape[1] // (tiles_first * block_size)
    per_second = right_rows.shape[1] // (tiles_second * block_size)
    tile_blocks = per_first * per_second
    left_blocks = left_rows.reshape(left_rows.shape[0], tiles_first * per_first, block_size)
    right_blocks = right_rows.reshape(right_rows.shape[0], tiles_second * per_second, block_size)

    def one_tile(inputs):
        first_index, tile_pattern = inputs
        usable = (tile_pattern < tile_blocks).astype(jnp.float32)
        clipped = jnp.minimum(tile_pattern, tile_blocks - 1)
        left_index = first_index * per_first + clipped // per_second
        right_index = jnp.arange(tiles_second, dtype=jnp.int32)[:, None] * per_second + clipped % per_second
        left_pick = jnp.take(left_blocks, left_index, axis=1).astype(jnp.float32)
        right_pick = jnp.take(right_blocks, right_index, axis=1).astype(jnp.float32)
        result = jnp.einsum("tbsi,tbsj->bsij", left_pick, right_pick)
        return result * usable[:, :, None, None]

    return lax.map(one_tile, (jnp.arange(tiles_first, dtype=jnp.int32), pattern))


def reference(tokens, upstream, w_gate, w_up, w_down, delta_gate, delta_up, delta_down, pattern_gate, pattern_up, pattern_down):
    gate_folded = fold_whole(w_gate, delta_gate, pattern_gate)
    up_folded = fold_whole(w_up, delta_up, pattern_up)
    down_folded = fold_whole(w_down, delta_down, pattern_down)
    gate_all = jnp.dot(tokens, gate_folded, preferred_element_type=jnp.float32)
    up_all = jnp.dot(tokens, up_folded, preferred_element_type=jnp.float32)
    sigmoid_all = jax.nn.sigmoid(gate_all)
    hidden = (gate_all * sigmoid_all * up_all).astype(jnp.bfloat16)
    output = jnp.dot(hidden, down_folded, preferred_element_type=jnp.float32).astype(jnp.bfloat16)
    backward = jnp.dot(upstream, down_folded.T, preferred_element_type=jnp.float32)
    grad_gate = (backward * up_all * sigmoid_all * (1.0 + gate_all * (1.0 - sigmoid_all))).astype(jnp.bfloat16)
    grad_up = (backward * gate_all * sigmoid_all).astype(jnp.bfloat16)
    input_grad = (jnp.dot(grad_gate, gate_folded.T, preferred_element_type=jnp.float32)
                  + jnp.dot(grad_up, up_folded.T, preferred_element_type=jnp.float32)).astype(jnp.bfloat16)
    delta_grad_gate = block_grads(tokens, grad_gate, pattern_gate)
    delta_grad_up = block_grads(tokens, grad_up, pattern_up)
    delta_grad_down = block_grads(hidden, upstream, pattern_down)
    return (output, input_grad, delta_grad_gate, delta_grad_up, delta_grad_down)
```

```python
import functools

import jax
import jax.numpy as jnp
from jax import lax
from jax.experimental import pallas as pl
from jax.experimental.pallas import tpu as pltpu
from jax.sharding import PartitionSpec as P


def divisor_up_to(total, limit):
    return max(size for size in range(1, limit + 1) if total % size == 0)


def fold_kernel(strips, column_blocks, block_size, slot_of, weight_ref, blocks_ref, out_ref):
    first = pl.program_id(0) * strips
    last_slot = blocks_ref.shape[0] - 1

    for strip in range(strips):
        rows = pl.ds(strip * block_size, block_size)

        def one_block(column, carry):
            slot = slot_of[(first + strip) * column_blocks + column]
            live = (slot >= 0).astype(jnp.float32)
            delta = blocks_ref[jnp.clip(slot, 0, last_slot)].astype(jnp.float32)
            columns = pl.ds(pl.multiple_of(column * block_size, block_size), block_size)
            total = weight_ref[rows, columns].astype(jnp.float32) + delta * live
            out_ref[rows, columns] = total.astype(out_ref.dtype)
            return carry

        lax.fori_loop(0, column_blocks, one_block, 0, unroll=2)


def fold_tile(weight, blocks, pattern):
    block_size = blocks.shape[-1]
    row_blocks = weight.shape[0] // block_size
    column_blocks = weight.shape[1] // block_size
    slot_list = pattern.reshape(-1)
    slots = slot_list.shape[0]
    flat_blocks = blocks.reshape(slots, block_size, block_size)
    numbers = jnp.arange(row_blocks * column_blocks, dtype=jnp.int32)
    hits = slot_list[:, None] == numbers[None, :]
    slot_of = jnp.max(jnp.where(hits, jnp.arange(slots, dtype=jnp.int32)[:, None], -1), axis=0)
    strips = divisor_up_to(row_blocks, 2)
    tile = pl.BlockSpec((strips * block_size, weight.shape[1]), lambda i, slot_of: (i, 0))
    return pl.pallas_call(
        functools.partial(fold_kernel, strips, column_blocks, block_size),
        grid_spec=pltpu.PrefetchScalarGridSpec(
            num_scalar_prefetch=1,
            grid=(row_blocks // strips,),
            in_specs=[tile, pl.BlockSpec(flat_blocks.shape, lambda i, slot_of: (0, 0, 0))],
            out_specs=tile,
        ),
        out_shape=jax.ShapeDtypeStruct(weight.shape, weight.dtype),
        compiler_params=pltpu.CompilerParams(vmem_limit_bytes=40 * 1024 * 1024),
        cost_estimate=pl.CostEstimate(
            flops=2 * weight.size,
            bytes_accessed=4 * weight.size + 2 * flat_blocks.size,
            transcendentals=0,
        ),
    )(slot_of, weight, flat_blocks)


def grads_kernel(group, right_count, tile_blocks, block_size, slots_ref, left_a, left_b, right_a, right_b, out_ref):
    first = pl.program_id(0) * group
    for index in range(group):
        block = slots_ref[first + index]
        live = (block < tile_blocks).astype(jnp.float32)
        block = jnp.minimum(block, tile_blocks - 1)
        above = block // right_count
        rows = pl.ds(pl.multiple_of(above * block_size, block_size), block_size)
        columns = pl.ds(
            pl.multiple_of((block - above * right_count) * block_size, block_size), block_size
        )
        total = jnp.dot(left_a[rows, :], right_a[:, columns], preferred_element_type=jnp.float32)
        total += jnp.dot(left_b[rows, :], right_b[:, columns], preferred_element_type=jnp.float32)
        out_ref[index] = total * live


def tile_grads(lefts, rights, slot_list, block_size):
    right_count = rights[0].shape[1] // block_size
    tile_blocks = (lefts[0].shape[0] // block_size) * right_count
    slots = slot_list.shape[0]
    group = divisor_up_to(slots, 8)
    whole = lambda array: pl.BlockSpec(array.shape, lambda i, slots_ref: (0, 0))
    return pl.pallas_call(
        functools.partial(grads_kernel, group, right_count, tile_blocks, block_size),
        grid_spec=pltpu.PrefetchScalarGridSpec(
            num_scalar_prefetch=1,
            grid=(slots // group,),
            in_specs=[whole(array) for array in (*lefts, *rights)],
            out_specs=pl.BlockSpec(
                (group, block_size, block_size), lambda i, slots_ref: (i, 0, 0)
            ),
        ),
        out_shape=jax.ShapeDtypeStruct((slots, block_size, block_size), jnp.float32),
        compiler_params=pltpu.CompilerParams(vmem_limit_bytes=40 * 1024 * 1024),
        cost_estimate=pl.CostEstimate(
            flops=16 * slots * block_size * block_size * lefts[0].shape[1],
            bytes_accessed=4 * slots * block_size * block_size
            + 4 * (lefts[0].size + rights[0].size),
            transcendentals=0,
        ),
    )(slot_list, *lefts, *rights)


def dot_transposed(left_rows, right_rows):
    return lax.dot_general(
        left_rows, right_rows, (((1,), (1,)), ((), ())), preferred_element_type=jnp.float32
    )


def to_pieces(left, right, contracted):
    return lax.dot_general(
        left, right, (contracted, ((), ())), preferred_element_type=jnp.float32
    ).astype(jnp.bfloat16)


def send_pieces(pieces, axis, count):
    rows = pieces.shape[0] // count
    me = lax.axis_index(axis)
    held = [lax.dynamic_slice_in_dim(pieces, me * rows, rows, 0)]
    for shift in range(1, count):
        target = lax.rem(me + shift, count)
        piece = lax.dynamic_slice_in_dim(pieces, target * rows, rows, 0)
        ring = [(source, (source + shift) % count) for source in range(count)]
        held.append(lax.ppermute(piece, axis, ring))
    return held


def sum_pieces(held):
    return functools.reduce(jnp.add, [piece.astype(jnp.float32) for piece in held])


def local(
    row_count,
    col_count,
    dp_count,
    tokens,
    upstream,
    w_gate,
    w_up,
    w_down,
    delta_gate,
    delta_up,
    delta_down,
    pattern_gate,
    pattern_up,
    pattern_down,
):
    block_size = delta_gate.shape[-1]
    swap = [(source, (source + 1) % dp_count) for source in range(dp_count)]

    def both(rows):
        return rows, lax.ppermute(rows, "dp", swap)

    def my_slots(pattern):
        slot_list = pattern.reshape(-1)
        mine = slot_list.shape[0] // dp_count
        return lax.dynamic_slice_in_dim(slot_list, lax.axis_index("dp") * mine, mine, 0)

    token_all = lax.all_gather(tokens, "row", axis=0, tiled=True)
    upstream_all = lax.all_gather(upstream, "row", axis=0, tiled=True)
    gate_folded = fold_tile(w_gate, delta_gate, pattern_gate)
    gate_pieces = to_pieces(token_all, gate_folded, ((1,), (0,)))
    gate_sent = send_pieces(gate_pieces, "col", col_count)
    w_up, _ = lax.optimization_barrier((w_up, gate_pieces))
    up_folded = fold_tile(w_up, delta_up, pattern_up)
    up_pieces = to_pieces(token_all, up_folded, ((1,), (0,)))
    up_sent = send_pieces(up_pieces, "col", col_count)
    w_down, _ = lax.optimization_barrier((w_down, up_pieces))
    down_folded = fold_tile(w_down, delta_down, pattern_down)
    backward_pieces = to_pieces(upstream_all, down_folded, ((1,), (1,)))
    token_columns = both(token_all.T)
    upstream_both = both(upstream_all)

    own_piece, backward_pieces = lax.optimization_barrier((gate_sent[0], backward_pieces))
    backward_sent = send_pieces(backward_pieces, "col", col_count)
    gate_mine = sum_pieces([own_piece, *gate_sent[1:]])
    up_mine = sum_pieces(up_sent)
    sigmoid_mine = jax.nn.sigmoid(gate_mine)
    hidden_mine = (gate_mine * sigmoid_mine * up_mine).astype(jnp.bfloat16)
    hidden_mine, gate_mine, up_mine = lax.optimization_barrier((hidden_mine, gate_mine, up_mine))
    hidden_all = lax.all_gather(hidden_mine, "col", axis=0, tiled=True)
    backward_mine = sum_pieces(backward_sent)
    sigmoid_mine = jax.nn.sigmoid(gate_mine)
    grad_gate = (
        backward_mine * up_mine * sigmoid_mine * (1.0 + gate_mine * (1.0 - sigmoid_mine))
    ).astype(jnp.bfloat16)
    grad_up = (backward_mine * gate_mine * sigmoid_mine).astype(jnp.bfloat16)
    grad_gate_all = lax.all_gather(grad_gate, "col", axis=0, tiled=True)
    grad_up_all = lax.all_gather(grad_up, "col", axis=0, tiled=True)

    output_terms = jnp.dot(hidden_all, down_folded, preferred_element_type=jnp.float32)
    output = lax.psum_scatter(output_terms, "row", scatter_dimension=0, tiled=True)
    output = output.astype(jnp.bfloat16)
    delta_grad_down = tile_grads(
        both(hidden_all.T), upstream_both, my_slots(pattern_down), block_size
    )
    gate_rows, delta_grad_down = lax.optimization_barrier((grad_gate_all, delta_grad_down))
    gate_part = dot_transposed(gate_rows, gate_folded)
    delta_grad_gate = tile_grads(
        token_columns, both(grad_gate_all), my_slots(pattern_gate), block_size
    )
    up_rows, gate_part, delta_grad_gate = lax.optimization_barrier(
        (grad_up_all, gate_part, delta_grad_gate)
    )
    input_grad = lax.psum_scatter(
        gate_part + dot_transposed(up_rows, up_folded), "row", scatter_dimension=0, tiled=True
    ).astype(jnp.bfloat16)
    delta_grad_up = tile_grads(token_columns, both(up_rows), my_slots(pattern_up), block_size)
    return (
        output,
        input_grad,
        delta_grad_gate[None, None],
        delta_grad_up[None, None],
        delta_grad_down[None, None],
    )


def solution(mesh):
    return jax.shard_map(
        functools.partial(local, mesh.shape["row"], mesh.shape["col"], mesh.shape["dp"]),
        mesh=mesh,
        in_specs=(
            P(("row", "dp"), "col"),
            P(("row", "dp"), "col"),
            P("col", "row"),
            P("col", "row"),
            P("row", "col"),
            P("col", "row", None, None, None),
            P("col", "row", None, None, None),
            P("row", "col", None, None, None),
            P("col", "row", None),
            P("col", "row", None),
            P("row", "col", None),
        ),
        out_specs=(
            P(("row", "dp"), "col"),
            P(("row", "dp"), "col"),
            P("col", "row", "dp", None, None),
            P("col", "row", "dp", None, None),
            P("row", "col", "dp", None, None),
        ),
        check_vma=False,
    )
```
